128 devices in a mesh: dp: 4 (over z_hi, core), seq: 32 (over x, y, z_lo).
Axes of the slice: x: 4, y: 4, z: 4 (z_hi: 2, z_lo: 2; z = z_hi * 2 + z_lo), core: 2. Of those that a mesh axis runs over, the one named last changes fastest.
Arguments:
- queries: bfloat16 [4, 4096, 1024], P('dp', 'seq'), may hold values from -40 to 40
- key_rows: bfloat16 [4, 4096, 1024], P('dp', 'seq'), may hold values from -9 to 9
- value_rows: bfloat16 [4, 4096, 1024], P('dp', 'seq'), may hold values from -6 to 6
- query_tangent: bfloat16 [4, 4096, 1024], P('dp', 'seq'), may hold values from -6 to 6
- key_tangent: bfloat16 [4, 4096, 1024], P('dp', 'seq'), may hold values from -6 to 6
- value_tangent: bfloat16 [4, 4096, 1024], P('dp', 'seq'), may hold values from -6 to 6
- out_weight: bfloat16 [1024, 2048], replicated, may hold values from -0.75 to 0.75
- upstream: bfloat16 [4, 4096, 2048], P('dp', 'seq'), may hold values from -6 to 6
Outputs:
- block_out: bfloat16 [4, 4096, 2048], P('dp', 'seq')
- tangent_out: bfloat16 [4, 4096, 2048], P('dp', 'seq')
- grad_weight: float32 [1024, 2048], P(('dp', 'seq'))
- grad_query: bfloat16 [4, 4096, 1024], P('dp', 'seq')
- grad_key: bfloat16 [4, 4096, 1024], P('dp', 'seq')
- grad_value: bfloat16 [4, 4096, 1024], P('dp', 'seq')
The draws below stay inside these ranges and needn't reach their ends.
All inputs are finite; a program needn't handle non-finite values.
Results may differ from the reference program's by a relative error of at most 0.035.
Values may be sent and summed in bfloat16 or wider, within the bound.
No kernel may reach another device: no remote copies, remote signals or barrier semaphores. Data moves between devices by JAX's collectives and lax.ppermute only.
A program may use at most 192 MiB of HBM per device.

```python
import math
import jax
import jax.numpy as jnp
from jax import lax

D = 2048
HEADS = 8
HEAD_DIM = 128
SEQ = 4096
BATCH = 4


def joint_draw(key):
    shape = (BATCH, SEQ, HEADS * HEAD_DIM)
    query_key = jax.random.fold_in(key, 11)
    keyed_key = jax.random.fold_in(key, 12)
    query_draw = jax.random.truncated_normal(query_key, -6.0, 6.0, shape, jnp.float32) * math.sqrt(2.0)
    key_draw = jax.random.truncated_normal(keyed_key, -6.0, 6.0, shape, jnp.float32) * math.sqrt(2.0)
    return (query_draw, key_draw)


def draw_queries(key, part):
    return joint_draw(key)[0].astype(jnp.bfloat16)


def draw_key_rows(key, part):
    return joint_draw(key)[1].astype(jnp.bfloat16)


def levels(rng, shape, split, smallest, top_value):
    gain, own = 1.0, jax.random.fold_in(rng, 6)
    for axis_at, parts in split:
        draws = jnp.exp(jax.random.uniform(jax.random.fold_in(own, axis_at), (parts,), jnp.float32, smallest / len(split), top_value / len(split)))
        gain = gain * jnp.repeat(draws, shape[axis_at] // parts).reshape([-1 if axis == axis_at else 1 for axis in range(len(shape))])
    return gain


def gaussian(stream_key, extent, width, limit, split=(), dtype=jnp.bfloat16):
    values = width * jax.random.normal(stream_key, extent, jnp.float32)
    if split:
        values = values * levels(stream_key, extent, split, -0.22, 0.18)
    return jnp.clip(values, -limit, limit).astype(dtype)


def setup_inputs(seed: int = 0) -> dict:
    arg_keys = jax.random.split(jax.random.key(seed), 9)
    return {
        "queries": draw_queries(jax.random.fold_in(arg_keys[8], 71), 0),
        "key_rows": draw_key_rows(jax.random.fold_in(arg_keys[8], 71), 0),
        "value_rows": gaussian(arg_keys[2], (BATCH, SEQ, HEADS * HEAD_DIM), 1.0, 6.0, ((0, 4), (1, 32))),
        "query_tangent": gaussian(arg_keys[3], (BATCH, SEQ, HEADS * HEAD_DIM), 1.0, 6.0, ((0, 4), (1, 32))),
        "key_tangent": gaussian(arg_keys[4], (BATCH, SEQ, HEADS * HEAD_DIM), 1.0, 6.0, ((0, 4), (1, 32))),
        "value_tangent": gaussian(arg_keys[5], (BATCH, SEQ, HEADS * HEAD_DIM), 1.0, 6.0, ((0, 4), (1, 32))),
        "out_weight": gaussian(arg_keys[6], (HEADS * HEAD_DIM, D), (HEADS * HEAD_DIM // 16) ** -0.5, 0.75),
        "upstream": gaussian(arg_keys[7], (BATCH, SEQ, D), 1.0, 6.0, ((0, 4), (1, 32))),
    }


def split_heads(matrix):
    return matrix.reshape(matrix.shape[0], HEADS, HEAD_DIM).transpose(1, 0, 2)

def join_heads(stacked):
    return stacked.transpose(1, 0, 2).reshape(stacked.shape[1], -1)

def head_forward(operands):
    query_head, key_head, value_head, query_tan, key_tan, value_tan = operands
    softmax_scale = HEAD_DIM ** (-0.5)
    scores = jnp.dot(query_head, key_head.T, preferred_element_type=jnp.float32) * softmax_scale
    tan_scores = (jnp.dot(query_tan, key_head.T, preferred_element_type=jnp.float32) + jnp.dot(query_head, key_tan.T, preferred_element_type=jnp.float32)) * softmax_scale
    row_max = lax.optimization_barrier(jnp.max(scores, axis=1, keepdims=True))
    exp_scores = jnp.exp(scores - row_max)
    weighted = exp_scores * tan_scores
    total = lax.optimization_barrier(jnp.sum(exp_scores, axis=1))
    tan_total = lax.optimization_barrier(jnp.sum(weighted, axis=1))
    exp_low = exp_scores.astype(jnp.bfloat16)
    main_acc = jnp.dot(exp_low, value_head, preferred_element_type=jnp.float32)
    tan_acc = jnp.dot(weighted.astype(jnp.bfloat16), value_head, preferred_element_type=jnp.float32) + jnp.dot(exp_low, value_tan, preferred_element_type=jnp.float32)
    attn_wide = main_acc / total[:, None]
    tan_attn = (tan_acc - attn_wide * tan_total[:, None]) / total[:, None]
    log_total = row_max[:, 0] + jnp.log(total)
    return (attn_wide.astype(jnp.bfloat16), tan_attn.astype(jnp.bfloat16), log_total)

def head_backward(operands):
    query_head, key_head, value_head, grad_head, attn_head, log_total = operands
    softmax_scale = HEAD_DIM ** (-0.5)
    scores = jnp.dot(query_head, key_head.T, preferred_element_type=jnp.float32) * softmax_scale
    attn_prob = jnp.exp(scores - log_total[:, None])
    grad_prob = jnp.dot(grad_head, value_head.T, preferred_element_type=jnp.float32)
    row_delta = lax.optimization_barrier(jnp.sum(grad_head.astype(jnp.float32) * attn_head.astype(jnp.float32), axis=1))
    grad_scores = (attn_prob * (grad_prob - row_delta[:, None])).astype(jnp.bfloat16)
    grad_query = (softmax_scale * jnp.dot(grad_scores, key_head, preferred_element_type=jnp.float32)).astype(jnp.bfloat16)
    grad_key = (softmax_scale * jnp.dot(grad_scores.T, query_head, preferred_element_type=jnp.float32)).astype(jnp.bfloat16)
    grad_value = jnp.dot(attn_prob.astype(jnp.bfloat16).T, grad_head, preferred_element_type=jnp.float32).astype(jnp.bfloat16)
    return (grad_query, grad_key, grad_value)

def one_sample(operands, out_weight):
    queries, key_rows, value_rows, query_tangent, key_tangent, value_tangent, upstream = operands
    forward_in = tuple((split_heads(matrix) for matrix in (queries, key_rows, value_rows, query_tangent, key_tangent, value_tangent)))
    attn_heads, tan_heads, log_total = lax.map(head_forward, forward_in)
    attn = join_heads(attn_heads)
    tan_attn = join_heads(tan_heads)
    block_wide = jnp.dot(attn, out_weight, preferred_element_type=jnp.float32)
    tan_wide = jnp.dot(tan_attn, out_weight, preferred_element_type=jnp.float32)
    cotangent = (tan_wide + upstream.astype(jnp.float32)).astype(jnp.bfloat16)
    grad_attn = jnp.dot(cotangent, out_weight.T, preferred_element_type=jnp.float32).astype(jnp.bfloat16)
    weight_part = jnp.dot(attn.T, cotangent, preferred_element_type=jnp.float32)
    backward_in = (split_heads(queries), split_heads(key_rows), split_heads(value_rows), split_heads(grad_attn), attn_heads, log_total)
    grads = lax.map(head_backward, backward_in)
    return (block_wide.astype(jnp.bfloat16), tan_wide.astype(jnp.bfloat16), weight_part, join_heads(grads[0]), join_heads(grads[1]), join_heads(grads[2]))

def reference(queries, key_rows, value_rows, query_tangent, key_tangent, value_tangent, out_weight, upstream):
    outputs = lax.map(lambda operands: one_sample(operands, out_weight), (queries, key_rows, value_rows, query_tangent, key_tangent, value_tangent, upstream))
    grad_weight = lax.optimization_barrier(jnp.sum(outputs[2], axis=0)) / math.sqrt(BATCH * SEQ)
    return (outputs[0], outputs[1], grad_weight, outputs[3], outputs[4], outputs[5])
```

```python
import functools
import math

import jax
import jax.numpy as jnp
from jax import lax
from jax.experimental import pallas as pl
from jax.experimental.pallas import tpu as pltpu
from jax.sharding import Mesh
from jax.sharding import PartitionSpec as P

HEADS = 8
HEAD_DIM = 128
SCALE = HEAD_DIM**-0.5
LOG2E = math.log2(math.e)
SHAPE = (2, 2, 4, 4, 2)
NAMES = ("zh", "core", "x", "y", "zl")
SEQ = ("x", "y", "zl")
HEAD_AXES = ("y", "zl")
BF16 = jnp.bfloat16
F32 = jnp.float32
VMEM_LIMIT = 60 * 1024 * 1024

NT = (((1,), (1,)), ((), ()))
NN = (((1,), (0,)), ((), ()))
TN = (((0,), (0,)), ((), ()))


def dot(a, b, dims):
    return lax.dot_general(a, b, dims, preferred_element_type=F32)


def params(**kw):
    return pltpu.CompilerParams(vmem_limit_bytes=VMEM_LIMIT, **kw)


def split_kernel(k, v, tk, tv, q, tq, kv_out, q_out):
    for x in range(kv_out.shape[0]):
        for at, ref in enumerate((k, tk, v, tv)):
            kv_out[x, 0, at] = ref[...]
    for at, ref in enumerate((q, tq)):
        q_out[0, at] = ref[...]


def split_heads(k, v, tk, tv, q, tq, copies):
    tokens = k.shape[0]
    part = pl.BlockSpec((tokens, HEAD_DIM), lambda h: (0, h))
    return pl.pallas_call(
        split_kernel,
        grid=(HEADS,),
        in_specs=[part] * 6,
        out_specs=[
            pl.BlockSpec((copies, 1, 4, tokens, HEAD_DIM), lambda h: (0, h, 0, 0, 0)),
            pl.BlockSpec((1, 2, tokens, HEAD_DIM), lambda h: (h, 0, 0, 0)),
        ],
        out_shape=[
            jax.ShapeDtypeStruct((copies, HEADS, 4, tokens, HEAD_DIM), BF16),
            jax.ShapeDtypeStruct((HEADS, 2, tokens, HEAD_DIM), BF16),
        ],
        name="split_heads",
    )(k, v, tk, tv, q, tq)


def forward_kernel(kv, q, exp_out, out, attn_t_out, stats_out, kk, vt, s_scr, w_scr, *, chunk):
    keys = s_scr.shape[0]
    sources, tokens = kv.shape[0], kv.shape[2]
    rows = s_scr.shape[1]

    @pl.when(pl.program_id(0) == 0)
    def _():
        for s in range(sources):
            at = pl.ds(s * tokens, tokens)
            kk[at, :HEAD_DIM] = kv[s, 0]
            kk[at, HEAD_DIM:] = kv[s, 1]
            vt[:HEAD_DIM, s * tokens : (s + 1) * tokens] = kv[s, 2].T
            vt[HEAD_DIM:, s * tokens : (s + 1) * tokens] = kv[s, 3].T

    q_blk = q[:, 0].reshape(rows, HEAD_DIM)
    tq_blk = q[:, 1].reshape(rows, HEAD_DIM)
    both = jnp.concatenate([tq_blk, q_blk], axis=1)
    top = jnp.full((8, rows), -jnp.inf, F32)
    for c in range(keys // chunk):
        at = pl.ds(c * chunk, chunk)
        s = dot(kk[at, :HEAD_DIM], q_blk, NT)
        s_scr[at, :] = s
        top = jnp.maximum(top, jnp.max(s.reshape(chunk // 8, 8, rows), axis=0))
    top = jnp.max(top, axis=0, keepdims=True)
    total = jnp.zeros((8, rows), F32)
    tan_total = jnp.zeros((8, rows), F32)
    for c in range(keys // chunk):
        at = pl.ds(c * chunk, chunk)
        e = jnp.exp2((s_scr[at, :] - top) * (SCALE * LOG2E))
        w = e * dot(kk[at, :], both, NT)
        total += jnp.sum(e.reshape(chunk // 8, 8, rows), axis=0)
        tan_total += jnp.sum(w.reshape(chunk // 8, 8, rows), axis=0)
        exp_out[at, :] = e.astype(BF16)
        w_scr[at, :] = w.astype(BF16)
    total = jnp.sum(total, axis=0, keepdims=True)
    tan_total = jnp.sum(tan_total, axis=0, keepdims=True) * SCALE
    ev = dot(vt[...], exp_out[...], NN)
    wv = dot(vt[:HEAD_DIM, :], w_scr[...], NN)
    inv = 1.0 / total
    wide = ev[:HEAD_DIM] * inv
    tan = (wv * SCALE + ev[HEAD_DIM:] - wide * tan_total) * inv
    attn = wide.astype(BF16)
    attn_t_out[...] = attn
    stats_out[...] = jnp.broadcast_to(inv, stats_out.shape)
    per = rows // tokens
    out[:, 0] = attn.T.reshape(per, tokens, HEAD_DIM)
    out[:, 1] = tan.astype(BF16).T.reshape(per, tokens, HEAD_DIM)


def forward(kv, q, rows=256, chunk=512):
    sources, _, tokens, _ = kv.shape
    keys = sources * tokens
    groups = q.shape[0]
    queries = groups * tokens
    per = rows // tokens
    return pl.pallas_call(
        functools.partial(forward_kernel, chunk=chunk),
        grid=(queries // rows,),
        in_specs=[
            pl.BlockSpec(kv.shape, lambda i: (0, 0, 0, 0)),
            pl.BlockSpec((per, 2, tokens, HEAD_DIM), lambda i: (i, 0, 0, 0)),
        ],
        out_specs=[
            pl.BlockSpec((keys, rows), lambda i: (0, i)),
            pl.BlockSpec((per, 2, tokens, HEAD_DIM), lambda i: (i, 0, 0, 0)),
            pl.BlockSpec((HEAD_DIM, rows), lambda i: (0, i)),
            pl.BlockSpec((8, rows), lambda i: (0, i)),
        ],
        out_shape=[
            jax.ShapeDtypeStruct((keys, queries), BF16),
            jax.ShapeDtypeStruct((groups, 2, tokens, HEAD_DIM), BF16),
            jax.ShapeDtypeStruct((HEAD_DIM, queries), BF16),
            jax.ShapeDtypeStruct((8, queries), F32),
        ],
        scratch_shapes=[
            pltpu.VMEM((keys, 2 * HEAD_DIM), BF16),
            pltpu.VMEM((2 * HEAD_DIM, keys), BF16),
            pltpu.VMEM((keys, rows), F32),
            pltpu.VMEM((keys, rows), BF16),
        ],
        compiler_params=params(),
        name="forward",
    )(kv, q)


def project_kernel(x, w, up, tan_out, cot_out, grad_out, attn_out, tan_scr):
    for h in range(HEADS):
        at = slice(h * HEAD_DIM, (h + 1) * HEAD_DIM)
        attn_out[:, at] = x[h, 0]
        tan_scr[:, at] = x[h, 1]
    ty = dot(tan_scr[...], w[...], NN)
    tan_out[...] = ty.astype(BF16)
    cot = (ty + up[...].astype(F32)).astype(BF16)
    cot_out[...] = cot
    grad = dot(cot, w[...], NT).astype(BF16)
    for h in range(HEADS):
        grad_out[h] = grad[:, h * HEAD_DIM : (h + 1) * HEAD_DIM]


def project(x, w, up):
    tokens = up.shape[0]
    return pl.pallas_call(
        project_kernel,
        out_shape=[
            jax.ShapeDtypeStruct(up.shape, BF16),
            jax.ShapeDtypeStruct(up.shape, BF16),
            jax.ShapeDtypeStruct((HEADS, tokens, HEAD_DIM), BF16),
            jax.ShapeDtypeStruct((tokens, HEADS * HEAD_DIM), BF16),
        ],
        scratch_shapes=[pltpu.VMEM((tokens, HEADS * HEAD_DIM), BF16)],
        compiler_params=params(),
        name="project",
    )(x, w, up)


def backward_kernel(exp_t, kv, q, grad, attn_t, stats, dkv_out, dq_out, acc, delta):
    step = pl.program_id(0)
    per, tokens = kv.shape[0], kv.shape[2]
    block = per * tokens
    queries = exp_t.shape[1]
    g = grad[...].reshape(queries, HEAD_DIM)

    @pl.when(step == 0)
    def _():
        acc[...] = jnp.zeros_like(acc)
        both = g.astype(F32).T * attn_t[...].astype(F32)
        delta[...] = jnp.broadcast_to(jnp.sum(both, axis=0, keepdims=True), delta.shape)

    q_all = q[:, 0].reshape(queries, HEAD_DIM)
    k_blk = kv[:, 0].reshape(block, HEAD_DIM)
    v_blk = kv[:, 2].reshape(block, HEAD_DIM)
    prob = exp_t[...].astype(F32) * stats[:1, :]
    dp = dot(v_blk, g, NT)
    ds = (prob * (dp - delta[:1, :])).astype(BF16)
    dk = dot(ds, q_all, NN) * SCALE
    dv = dot(prob.astype(BF16), g, NN)
    dkv_out[:, 0] = dk.astype(BF16).reshape(per, tokens, HEAD_DIM)
    dkv_out[:, 1] = dv.astype(BF16).reshape(per, tokens, HEAD_DIM)
    acc[...] += dot(k_blk, ds, TN)

    @pl.when(step == pl.num_programs(0) - 1)
    def _():
        dq_out[...] = (acc[...] * SCALE).astype(BF16).T.reshape(dq_out.shape)


def backward(exp_t, kv, q, grad, attn_t, stats, block=512):
    sources, _, tokens, _ = kv.shape
    keys, queries = exp_t.shape
    per = block // tokens
    groups = q.shape[0]
    whole = lambda a: pl.BlockSpec(a.shape, lambda i: (0,) * a.ndim)
    return pl.pallas_call(
        backward_kernel,
        grid=(keys // block,),
        in_specs=[
            pl.BlockSpec((block, queries), lambda i: (i, 0)),
            pl.BlockSpec((per, 4, tokens, HEAD_DIM), lambda i: (i, 0, 0, 0)),
            whole(q),
            whole(grad),
            whole(attn_t),
            whole(stats),
        ],
        out_specs=[
            pl.BlockSpec((per, 2, tokens, HEAD_DIM), lambda i: (i, 0, 0, 0)),
            pl.BlockSpec((groups, tokens, HEAD_DIM), lambda i: (0, 0, 0)),
        ],
        out_shape=[
            jax.ShapeDtypeStruct((sources, 2, tokens, HEAD_DIM), BF16),
            jax.ShapeDtypeStruct((groups, tokens, HEAD_DIM), BF16),
        ],
        scratch_shapes=[
            pltpu.VMEM((HEAD_DIM, queries), F32),
            pltpu.VMEM((8, queries), F32),
        ],
        compiler_params=params(),
        name="backward",
    )(exp_t, kv, q, grad, attn_t, stats)


def join_kernel(dkv, dq, dk_out, dv_out, dq_out):
    terms = dkv[...].astype(F32)
    total = jnp.sum(terms, axis=0)[0]
    dk_out[...] = total[0].astype(BF16)
    dv_out[...] = total[1].astype(BF16)
    dq_out[...] = dq[0]


def join_heads(dkv, dq):
    copies, _, _, tokens, _ = dkv.shape
    part = pl.BlockSpec((tokens, HEAD_DIM), lambda h: (0, h))
    shape = jax.ShapeDtypeStruct((tokens, HEADS * HEAD_DIM), BF16)
    return pl.pallas_call(
        join_kernel,
        grid=(HEADS,),
        in_specs=[
            pl.BlockSpec((copies, 1, 2, tokens, HEAD_DIM), lambda h: (0, h, 0, 0, 0)),
            pl.BlockSpec((1, tokens, HEAD_DIM), lambda h: (h, 0, 0)),
        ],
        out_specs=[part] * 3,
        out_shape=[shape] * 3,
        name="join_heads",
    )(dkv, dq)


def exchange(value, axes):
    return lax.all_to_all(value, axes, 0, 0, tiled=True)


def weight_gradient(attn, cot):
    tokens, width = attn.shape
    core = lax.axis_index("core")
    swap = [(0, 1), (1, 0)]
    halves = attn.reshape(tokens, 2, 2, width // 4)
    lower, upper = halves[:, :, 0], halves[:, :, 1]
    mine = jnp.where(core == 0, lower, upper)
    theirs = lax.ppermute(jnp.where(core == 0, upper, lower), "core", swap)
    their_cot = lax.ppermute(cot, "core", swap)
    rows = jnp.concatenate([mine, theirs], axis=0).reshape(2 * tokens, width // 2)
    part = dot(rows, jnp.concatenate([cot, their_cot], axis=0), TN).astype(BF16)
    peers = lax.axis_size(("zh", "x", "y", "zl"))
    part = part.reshape(peers, width // (2 * peers), cot.shape[1])
    got = exchange(part, ("zh", "x", "y", "zl"))
    count = tokens * peers * 2
    return jnp.sum(got.astype(F32), axis=0) * (1.0 / math.sqrt(count))


def per_device(q, k, v, tq, tk, tv, weight, upstream):
    tokens, width = q.shape[1], q.shape[2]
    copies = lax.axis_size("x")
    kv_send, q_send = split_heads(k[0], v[0], tk[0], tv[0], q[0], tq[0], copies)
    q_all = exchange(q_send, HEAD_AXES)
    kv_all = exchange(kv_send.reshape(copies * HEADS, 4, tokens, HEAD_DIM), SEQ)
    exp_t, heads_out, attn_t, stats = forward(kv_all, q_all)
    owned = exchange(heads_out, HEAD_AXES)
    tan_out, cot, grad_send, attn = project(owned, weight, upstream[0])
    grad = exchange(grad_send, HEAD_AXES)
    block_out = dot(attn, weight, NN).astype(BF16)
    grad_weight = weight_gradient(attn, cot)
    dkv, dq = backward(exp_t, kv_all, q_all, grad, attn_t, stats)
    dq_all = exchange(dq, HEAD_AXES)
    dkv_all = exchange(dkv, SEQ).reshape(copies, HEADS, 2, tokens, HEAD_DIM)
    grad_key, grad_value, grad_query = join_heads(dkv_all, dq_all)
    return (
        block_out[None],
        tan_out[None],
        grad_weight,
        grad_query[None],
        grad_key[None],
        grad_value[None],
    )


def solution(mesh):
    parts = Mesh(mesh.devices.reshape(SHAPE), NAMES)
    tokens = P(("zh", "core"), SEQ, None)
    return jax.shard_map(
        per_device,
        mesh=parts,
        in_specs=(tokens,) * 6 + (P(), tokens),
        out_specs=(tokens, tokens, P(("zh", "core") + SEQ, None), tokens, tokens, tokens),
        check_vma=False,
    )
```
